512 devices in a mesh: ia: 64 (over x, z_lo, core), jb: 8 (over y, z_hi).
Axes of the slice: x: 4, y: 4, z: 16 (z_hi: 2, z_lo: 8; z = z_hi * 8 + z_lo), core: 2. Of those that a mesh axis runs over, the one named last changes fastest.
Arguments:
- density: bfloat16 [8000, 100000], P('ia', 'jb'), may hold values from -6 to 6
- chol_vectors: bfloat16 [100000, 512], P('jb', 'ia'), may hold values from -0.01953125 to 0.01953125
- virt_coef: bfloat16 [1000, 1100], P('jb'), may hold values from -0.1875 to 0.1875
Outputs:
- half_back: float32 [8, 512, 1100], P(None, ('ia', 'jb'))
The draws below stay inside these ranges and needn't reach their ends.
All inputs are finite; a program needn't handle non-finite values.
Results may differ from the reference program's by a relative error of at most 0.0003.
Values may be sent and summed in bfloat16 or wider, within the bound.
No kernel may reach another device: no remote copies, remote signals or barrier semaphores. Data moves between devices by JAX's collectives and lax.ppermute only.
A program may use at most 64 MiB of HBM per device.

```python
import jax
import jax.numpy as jnp
from jax import lax

NOCC = 100
NV = 1000
NAO = 1100
OSLAB = 8
NCHOL = 512


def level_of(rng, extent, cuts, smallest, high):
    level, own = 1.0, jax.random.fold_in(rng, 6)
    for dim, shards_of in cuts:
        heights = jnp.exp(jax.random.uniform(jax.random.fold_in(own, dim), (shards_of,), jnp.float32, smallest / len(cuts), high / len(cuts)))
        level = level * jnp.repeat(heights, extent[dim] // shards_of).reshape([-1 if axis == dim else 1 for axis in range(len(extent))])
    return level


def noise(stream_key, shape, scale, most, cuts=(), dtype=jnp.bfloat16):
    entries = jax.random.normal(stream_key, shape, jnp.float32) * scale
    if len(cuts) > 0:
        entries = level_of(stream_key, shape, cuts, -0.22, 0.18) * entries
    return jnp.clip(entries, min=-most, max=most).astype(dtype)


def setup_inputs(seed: int = 0) -> dict:
    keys = jax.random.split(jax.random.key(seed), 4)
    return {
        "density": noise(keys[0], (OSLAB * NV, NOCC * NV), 1.0, 6.0, ((0, 64), (1, 8))),
        "chol_vectors": noise(keys[1], (NOCC * NV, NCHOL), (NOCC * NV) ** -0.5, 0.01953125, ((0, 8), (1, 64))),
        "virt_coef": noise(keys[2], (NV, NAO), NV ** -0.5, 0.1875, ((0, 8),)),
    }


def reference(density, chol_vectors, virt_coef):
    gamma_full = jnp.dot(density, chol_vectors, preferred_element_type=jnp.float32)
    gamma_full = gamma_full.reshape(OSLAB, NV, NCHOL)
    return jnp.einsum("iap,an->ipn", gamma_full, virt_coef.astype(jnp.float32), precision=lax.Precision.HIGHEST)
```

```python
import jax
import jax.numpy as jnp
from jax import lax
from jax.experimental import pallas as pl
from jax.experimental.pallas import tpu as pltpu
from jax.sharding import Mesh
from jax.sharding import PartitionSpec as P


AXES = ("x", "zl", "c", "y", "zh")
X, ZL, C, Y, ZH = 4, 8, 2, 4, 2
FOLD = (0, 2, 4, 6, 7, 5, 3, 1)
STEPS = (0, -1, 1, -2, 2, -3, 3, 4)
SHIFTS = (0, 1, 3, 2)
LANES = 128


def fold_ring(step):
    return [(FOLD[i], FOLD[(i + step) % ZL]) for i in range(ZL)]


def swap(shard, axis):
    return lax.ppermute(shard, axis, [(0, 1), (1, 0)])


def exchange(shard, axes):
    return lax.all_to_all(shard, axes, split_axis=0, concat_axis=0, tiled=True)


def gathered(shard, axes, count):
    return exchange(jnp.broadcast_to(shard[None], (count,) + shard.shape), axes)


def ring_gather(piece):
    parts = [piece]
    up, down = piece, piece
    for _ in range(1, ZL // 2):
        up = lax.ppermute(up, "zl", fold_ring(1))
        down = lax.ppermute(down, "zl", fold_ring(-1))
        parts += [up, down]
    half = piece.shape[0] // 2
    first = lax.ppermute(up[:half], "zl", fold_ring(1))
    second = lax.ppermute(down[half:], "zl", fold_ring(-1))
    return parts + [first, second]


def ring_source(step):
    here = lax.axis_index("zl")
    place = jnp.where(lax.rem(here, 2) == 0, here // 2, (2 * ZL - 1 - here) // 2)
    place = lax.rem(place + step + ZL, ZL)
    return jnp.where(place < ZL // 2, 2 * place, 2 * ZL - 1 - 2 * place)


def contract_kernel(*refs):
    parts, pieces, (_, out, acc) = refs[: ZL + 1], refs[ZL + 1 : ZL + 1 + 2 * X], refs[ZL + 1 + 2 * X :]
    index = pl.program_id(0)
    width = parts[0].shape[0]
    rows = pieces[0].shape[1]

    @pl.when(index == 0)
    def _():
        acc[...] = jnp.zeros_like(acc)

    left = jnp.concatenate([part[...] for part in parts], axis=0)
    for slot, piece in enumerate(pieces):
        source = lax.rem(lax.axis_index("x") - SHIFTS[slot // 2] + X, X)
        acc[2 * source + slot % 2, :, :rows] += jnp.dot(left, piece[...], preferred_element_type=jnp.float32)

    @pl.when(index == pl.num_programs(0) - 1)
    def _():
        for piece in range(2 * X):
            for slot in range(ZL):
                for part in range(2):
                    for owner in range(ZH):
                        got = acc[piece, pl.ds(slot * width + part * 16 + owner, 8, stride=2), :]
                        start = part * 1024 + (slot * ZH + owner) * 8 + piece
                        out[pl.ds(start, 8, stride=LANES), :] = got


def contract(parts, pieces, ready):
    width, quarter = parts[0].shape
    rows = pieces[0].shape[1]
    columns = ZL * width
    block = 5 * LANES
    lefts = [pl.BlockSpec((part.shape[0], block), lambda k: (0, k)) for part in parts]
    rights = [pl.BlockSpec((block, rows), lambda k: (k, 0))] * len(pieces)
    return pl.pallas_call(
        contract_kernel,
        grid=(quarter // block,),
        out_shape=jax.ShapeDtypeStruct((columns * 2 * X, LANES), jnp.float32),
        in_specs=lefts + rights + [pl.BlockSpec(memory_space=pl.ANY)],
        out_specs=pl.BlockSpec((columns * 2 * X, LANES), lambda k: (0, 0)),
        scratch_shapes=[pltpu.VMEM((2 * X, columns, LANES), jnp.float32)],
        cost_estimate=pl.CostEstimate(
            flops=2 * columns * quarter * 2 * X * LANES, bytes_accessed=8 << 20, transcendentals=0
        ),
        name="contract",
    )(*parts, *pieces, ready)


def regroup_kernel(got, out):
    for slot in range(ZL):
        target = ring_source(STEPS[slot])
        for owner in range(ZH):
            tile = slot * ZH + owner
            total = got[0, tile]
            for source in range(1, X * Y):
                total += got[source, tile]
            out[owner, target] = total


def regroup(got):
    return pl.pallas_call(
        regroup_kernel,
        out_shape=jax.ShapeDtypeStruct((ZH, ZL, 2 * X, LANES), jnp.float32),
        cost_estimate=pl.CostEstimate(flops=1 << 18, bytes_accessed=1 << 20, transcendentals=0),
        name="regroup",
    )(got)


def on_device(density, chol_vectors, virt_coef):
    rows, inner = density.shape
    width = chol_vectors.shape[1]
    virt_rows, nao = virt_coef.shape
    core, half = lax.axis_index("c"), lax.axis_index("zh")
    block = 5 * LANES
    quarter = -(-inner // (X * block)) * block
    pad = X * quarter - inner

    vectors = jnp.pad(chol_vectors.T, ((0, 0), (0, pad))).reshape(width, X, quarter)
    vectors = exchange(vectors.transpose(1, 0, 2), "x").reshape(X * width, quarter)
    parts = ring_gather(vectors)

    dens = jnp.pad(density.T, ((0, pad), (0, 0)))
    pieces = []
    for shift in SHIFTS:
        start = lax.rem(lax.axis_index("x") + shift, X) * quarter
        piece = lax.dynamic_slice(dens, (start, 0), (quarter, rows))
        if shift:
            piece = lax.ppermute(piece, "x", [(i, (i + shift) % X) for i in range(X)])
        pieces += [piece, swap(piece, "c")]

    coef = virt_coef.T
    part = -(-nao // (X * C * 16)) * 16
    coef = jnp.pad(coef, ((0, X * C * part - nao), (0, LANES - virt_rows)))
    mine = lax.axis_index("x") * C + core
    far = swap(lax.dynamic_slice(coef, (mine * part, 0), (part, LANES)), "zh")
    far = gathered(far, ("x", "c"), X * C).reshape(X * C * part, LANES)
    pair = jnp.where(half == core, jnp.stack([coef, far]), jnp.stack([far, coef]))
    coefs = gathered(pair, "y", Y)

    gamma = contract(parts, pieces, coefs)
    gamma = exchange(gamma.reshape(X * Y, ZL * ZH * 2 * X, LANES), ("x", "y"))
    gamma = regroup(gamma.reshape(X * Y, ZL * ZH, 2 * X, LANES))
    gamma = exchange(gamma.reshape(ZH * ZL, 2 * X, LANES), ("zh", "zl"))
    gamma = jnp.sum(gamma.reshape(ZH, 2, ZL // 2, X, 2, LANES), axis=0)
    gamma = gamma.transpose(2, 0, 1, 3, 4).reshape(2 * X, ZL // 2 * 2, LANES)
    out = jnp.einsum(
        "ibr,bnr->in",
        gamma,
        coefs.reshape(2 * Y, X * C * part, LANES).astype(jnp.float32),
        precision=lax.Precision.HIGHEST,
    )
    return out[:, None, :nao]


def solution(mesh):
    split = Mesh(mesh.devices.reshape(X, ZL, C, Y, ZH), AXES)
    return jax.shard_map(
        on_device,
        mesh=split,
        in_specs=(P(("x", "zl", "c"), ("y", "zh")), P(("y", "zh"), ("x", "zl", "c")), P(("y", "zh"), None)),
        out_specs=P(None, AXES, None),
        check_vma=False,
    )
```

```python
import jax
import jax.numpy as jnp
from jax import lax
from jax.experimental import pallas as pl
from jax.experimental.pallas import tpu as pltpu
from jax.sharding import Mesh
from jax.sharding import PartitionSpec as P


AXES = ("x", "zl", "c", "y", "zh")
X, ZL, C, Y, ZH = 4, 8, 2, 4, 2
FOLD = (0, 2, 4, 6, 7, 5, 3, 1)
STEPS = (0, -1, 1, -2, 2, -3, 3, 4)
PAIR = [(0, 1), (1, 0), (2, 3), (3, 2)]
CROSS = [(1, 2), (2, 1), (3, 0), (0, 3)]
LANES = 128
BLOCK = 10 * LANES
PIECES = 4


def fold_ring(step):
    return [(FOLD[i], FOLD[(i + step) % ZL]) for i in range(ZL)]


def swap(shard, axis):
    return lax.ppermute(shard, axis, [(0, 1), (1, 0)])


def exchange(shard, axes):
    return lax.all_to_all(shard, axes, split_axis=0, concat_axis=0, tiled=True)


def gathered(shard, axes, count):
    return exchange(jnp.broadcast_to(shard[None], (count,) + shard.shape), axes)


def ring_gather(piece):
    parts = [piece]
    up, down = piece, piece
    for _ in range(1, ZL // 2):
        up = lax.ppermute(up, "zl", fold_ring(1))
        down = lax.ppermute(down, "zl", fold_ring(-1))
        parts += [up, down]
    half = piece.shape[0] // 2
    first = lax.ppermute(up[:half], "zl", fold_ring(1))
    second = lax.ppermute(down[half:], "zl", fold_ring(-1))
    return parts + [first, second]


def ring_source(step):
    here = lax.axis_index("zl")
    place = jnp.where(lax.rem(here, 2) == 0, here // 2, (2 * ZL - 1 - here) // 2)
    place = lax.rem(place + step + ZL, ZL)
    return jnp.where(place < ZL // 2, 2 * place, 2 * ZL - 1 - 2 * place)


def contract_kernel(*refs):
    own, cross, (a, b, c, d, _, out, acc) = refs[: ZL + 1], refs[ZL + 1 : ZL + 4], refs[ZL + 4 :]
    index = pl.program_id(0)
    here = lax.axis_index("x")

    @pl.when(index == 0)
    def _():
        acc[...] = jnp.zeros_like(acc)

    own = jnp.concatenate([part[...] for part in own], axis=0)
    cross = jnp.concatenate([part[...] for part in cross], axis=0)
    low = here < X // 2
    left = jnp.concatenate([jnp.where(low, own, cross), jnp.where(low, cross, own)], axis=0)
    even = lax.rem(here, 2) == 0
    one = jnp.concatenate([a[...], b[...]], axis=1)
    two = jnp.concatenate([c[...], d[...]], axis=1)
    for slot, right in enumerate((jnp.where(even, one, two), jnp.where(even, two, one))):
        both = jnp.dot(left, right, preferred_element_type=jnp.float32)
        acc[2 * slot] += both[:, :LANES]
        acc[2 * slot + 1] += both[:, LANES:]

    @pl.when(index == pl.num_programs(0) - 1)
    def _():
        for piece in range(PIECES):
            for half in range(2):
                for slot in range(ZL):
                    for owner in range(ZH):
                        got = acc[piece, pl.ds((half * ZL + slot) * 16 + owner, 8, stride=2), :]
                        start = half * 512 + (slot * ZH + owner) * PIECES + piece
                        out[pl.ds(start, 8, stride=ZL * ZH * PIECES), :] = got


def contract(own, cross, pieces, ready):
    inner = own[0].shape[1]
    columns = X * ZL * own[0].shape[0] // 2
    lefts = [pl.BlockSpec((part.shape[0], BLOCK), lambda k: (0, k)) for part in own + cross]
    rights = [pl.BlockSpec((BLOCK, LANES), lambda k: (k, 0))] * len(pieces)
    return pl.pallas_call(
        contract_kernel,
        grid=(inner // BLOCK,),
        out_shape=jax.ShapeDtypeStruct((columns * PIECES, LANES), jnp.float32),
        in_specs=lefts + rights + [pl.BlockSpec(memory_space=pl.ANY)],
        out_specs=pl.BlockSpec((columns * PIECES, LANES), lambda k: (0, 0)),
        scratch_shapes=[pltpu.VMEM((PIECES, columns, LANES), jnp.float32)],
        cost_estimate=pl.CostEstimate(
            flops=2 * columns * inner * PIECES * LANES, bytes_accessed=10 << 20, transcendentals=0
        ),
        name="contract",
    )(*own, *cross, *pieces, ready)


def regroup_kernel(got, out):
    for slot in range(ZL):
        target = ring_source(STEPS[slot])
        for pair in range(2):
            total = got[pair * 2 * Y, slot]
            for source in range(pair * 2 * Y + 1, (pair + 1) * 2 * Y):
                total += got[source, slot]
            for owner in range(ZH):
                out[owner, target, pair * PIECES : (pair + 1) * PIECES, :] = total[
                    owner * PIECES : (owner + 1) * PIECES
                ]


def regroup(got):
    return pl.pallas_call(
        regroup_kernel,
        out_shape=jax.ShapeDtypeStruct((ZH, ZL, 2 * X, LANES), jnp.float32),
        cost_estimate=pl.CostEstimate(flops=1 << 17, bytes_accessed=1 << 19, transcendentals=0),
        name="regroup",
    )(got)


def on_device(density, chol_vectors, virt_coef):
    rows, inner = density.shape
    width = chol_vectors.shape[1]
    virt_rows, nao = virt_coef.shape
    here, core, half = lax.axis_index("x"), lax.axis_index("c"), lax.axis_index("zh")
    even = lax.rem(here, 2) == 0
    depth = -(-inner // (2 * BLOCK)) * BLOCK
    pad = 2 * depth - inner
    keep = lax.rem((here + 1) // 2, 2)
    keep, give = keep * depth, (1 - keep) * depth

    vectors = jnp.pad(chol_vectors.T, ((0, 0), (0, pad)))
    mine = lax.dynamic_slice(vectors, (0, keep), (width, depth))
    sent = lax.dynamic_slice(vectors, (0, give), (width, depth))
    got = lax.ppermute(sent, "x", PAIR)
    chunk = jnp.concatenate([jnp.where(even, mine, got), jnp.where(even, got, mine)], axis=0)
    own = ring_gather(chunk)
    cross = [
        lax.ppermute(jnp.concatenate(own[first:last], axis=0), "x", CROSS)
        for first, last in ((0, 3), (3, 5), (5, 9))
    ]

    dens = jnp.pad(density.T, ((0, pad), (0, LANES - rows)))
    kept = lax.dynamic_slice(dens, (keep, 0), (depth, LANES))
    other = lax.ppermute(lax.dynamic_slice(dens, (give, 0), (depth, LANES)), "x", PAIR)
    pieces = [kept, swap(kept, "c"), other, swap(other, "c")]

    coef = virt_coef.T
    part = -(-nao // (X * C * 16)) * 16
    coef = jnp.pad(coef, ((0, X * C * part - nao), (0, LANES - virt_rows)))
    far = lax.dynamic_slice(coef, ((here * C + core) * part, 0), (part, LANES))
    far = swap(far, "zh")
    far = gathered(far, ("x", "c"), X * C).reshape(X * C * part, LANES)
    pair = jnp.where(half == core, jnp.stack([coef, far]), jnp.stack([far, coef]))
    coefs = gathered(pair, "y", Y)

    gamma = contract(own, cross, pieces, coefs[0, 0, :16])
    gamma = exchange(gamma.reshape(X * Y, ZL * ZH * PIECES, LANES), ("x", "y"))
    gamma = regroup(gamma.reshape(X * Y, ZL, ZH * PIECES, LANES))
    gamma = exchange(gamma.reshape(ZH * ZL, 2 * X, LANES), ("zh", "zl"))
    gamma = jnp.sum(gamma.reshape(ZH, 2, ZL // 2, X, 2, LANES), axis=0)
    gamma = gamma.transpose(2, 0, 1, 3, 4).reshape(2 * X, ZL // 2 * 2, LANES)
    out = jnp.einsum(
        "ibr,bnr->in",
        gamma,
        coefs.reshape(2 * Y, X * C * part, LANES).astype(jnp.float32),
        precision=lax.Precision.HIGHEST,
    )
    return out[:, None, :nao]


def solution(mesh):
    split = Mesh(mesh.devices.reshape(X, ZL, C, Y, ZH), AXES)
    return jax.shard_map(
        on_device,
        mesh=split,
        in_specs=(P(("x", "zl", "c"), ("y", "zh")), P(("y", "zh"), ("x", "zl", "c")), P(("y", "zh"), None)),
        out_specs=P(None, AXES, None),
        check_vma=False,
    )
```

```python
import jax
import jax.numpy as jnp
from jax import lax
from jax.experimental import pallas as pl
from jax.experimental.pallas import tpu as pltpu
from jax.sharding import Mesh
from jax.sharding import PartitionSpec as P


AXES = ("x", "zl", "c", "y", "zh")
X, ZL, C, Y, ZH = 4, 8, 2, 4, 2
FOLD = (0, 2, 4, 6, 7, 5, 3, 1)
STEPS = (0, -1, 1, -2, 2, -3, 3, 4)
PAIR = [(0, 1), (1, 0), (2, 3), (3, 2)]
CROSS = [(1, 2), (2, 1), (3, 0), (0, 3)]
LANES = 128
BLOCK = 10 * LANES
PIECES = 4


def fold_ring(step):
    return [(FOLD[i], FOLD[(i + step) % ZL]) for i in range(ZL)]


def swap(shard, axis):
    return lax.ppermute(shard, axis, [(0, 1), (1, 0)])


def exchange(shard, axes):
    return lax.all_to_all(shard, axes, split_axis=0, concat_axis=0, tiled=True)


def gathered(shard, axes, count):
    return exchange(jnp.broadcast_to(shard[None], (count,) + shard.shape), axes)


def ring_gather(piece):
    parts = [piece]
    up, down = piece, piece
    for _ in range(1, ZL // 2):
        up = lax.ppermute(up, "zl", fold_ring(1))
        down = lax.ppermute(down, "zl", fold_ring(-1))
        parts += [up, down]
    return parts + [lax.ppermute(up, "zl", fold_ring(1))]


def ring_source(step):
    here = lax.axis_index("zl")
    place = jnp.where(lax.rem(here, 2) == 0, here // 2, (2 * ZL - 1 - here) // 2)
    place = lax.rem(place + step + ZL, ZL)
    return jnp.where(place < ZL // 2, 2 * place, 2 * ZL - 1 - 2 * place)


def contract_kernel(*refs):
    own, cross, (a, b, c, d, out, acc) = refs[:ZL], refs[ZL : ZL + 4], refs[ZL + 4 :]
    index = pl.program_id(0)
    here = lax.axis_index("x")

    @pl.when(index == 0)
    def _():
        acc[...] = jnp.zeros_like(acc)

    own = jnp.concatenate([part[...] for part in own], axis=0)
    cross = jnp.concatenate([part[...] for part in cross], axis=0)
    low = here < X // 2
    left = jnp.concatenate([jnp.where(low, own, cross), jnp.where(low, cross, own)], axis=0)
    even = lax.rem(here, 2) == 0
    one = jnp.concatenate([a[...], b[...]], axis=1)
    two = jnp.concatenate([c[...], d[...]], axis=1)
    for slot, right in enumerate((jnp.where(even, one, two), jnp.where(even, two, one))):
        both = jnp.dot(left, right, preferred_element_type=jnp.float32)
        acc[2 * slot] += both[:, :LANES]
        acc[2 * slot + 1] += both[:, LANES:]

    @pl.when(index == pl.num_programs(0) - 1)
    def _():
        for piece in range(PIECES):
            for half in range(2):
                for slot in range(ZL):
                    for owner in range(ZH):
                        got = acc[piece, pl.ds((half * ZL + slot) * 16 + owner, 8, stride=2), :]
                        start = half * 512 + (slot * ZH + owner) * PIECES + piece
                        out[pl.ds(start, 8, stride=ZL * ZH * PIECES), :] = got


def contract(own, cross, pieces):
    inner = own[0].shape[1]
    columns = X * ZL * own[0].shape[0] // 2
    lefts = [pl.BlockSpec((part.shape[0], BLOCK), lambda k: (0, k)) for part in own + cross]
    rights = [pl.BlockSpec((BLOCK, LANES), lambda k: (k, 0))] * len(pieces)
    return pl.pallas_call(
        contract_kernel,
        grid=(inner // BLOCK,),
        out_shape=jax.ShapeDtypeStruct((columns * PIECES, LANES), jnp.float32),
        in_specs=lefts + rights,
        out_specs=pl.BlockSpec((columns * PIECES, LANES), lambda k: (0, 0)),
        scratch_shapes=[pltpu.VMEM((PIECES, columns, LANES), jnp.float32)],
        cost_estimate=pl.CostEstimate(
            flops=2 * columns * inner * PIECES * LANES, bytes_accessed=10 << 20, transcendentals=0
        ),
        name="contract",
    )(*own, *cross, *pieces)


def regroup_kernel(got, out):
    for slot in range(ZL):
        target = ring_source(STEPS[slot])
        for pair in range(2):
            total = got[pair * 2 * Y, slot]
            for source in range(pair * 2 * Y + 1, (pair + 1) * 2 * Y):
                total += got[source, slot]
            for owner in range(ZH):
                out[owner, target, pair * PIECES : (pair + 1) * PIECES, :] = total[
                    owner * PIECES : (owner + 1) * PIECES
                ]


def regroup(got):
    return pl.pallas_call(
        regroup_kernel,
        out_shape=jax.ShapeDtypeStruct((ZH, ZL, 2 * X, LANES), jnp.float32),
        cost_estimate=pl.CostEstimate(flops=1 << 17, bytes_accessed=1 << 19, transcendentals=0),
        name="regroup",
    )(got)


def transform_kernel(got, *refs):
    coefs, out = refs[:Y], refs[Y]
    nao = out.shape[2]
    here = lax.axis_index("y")
    totals = [0.0, 0.0]
    for coef, shift in zip(coefs, (0, 1, 3, 2)):
        block = lax.rem(here - shift + Y, Y)
        tiles = [got[Y * h + block] + got[ZL + Y * h + block] for h in range(2)]
        rest = jnp.concatenate(tiles, axis=0)
        terms = []
        for _ in range(3):
            terms.append(rest.astype(jnp.bfloat16))
            rest = rest - terms[-1].astype(jnp.float32)
        terms = jnp.concatenate(terms, axis=0)
        for side in range(2):
            part = lax.dot_general(
                terms, coef[side], (((1,), (1,)), ((), ())), preferred_element_type=jnp.float32
            )
            totals[side] += (part[:16] + part[16:32]) + part[32:]
    for source in range(X):
        for h in range(2):
            row = h * 2 * X + 2 * source
            line = totals[0][row : row + 1] + totals[1][row + 1 : row + 2]
            out[2 * source + h] = line[:, :nao]


def transform(got, coefs, nao):
    vmem = pl.BlockSpec(memory_space=pltpu.VMEM)
    return pl.pallas_call(
        transform_kernel,
        out_shape=jax.ShapeDtypeStruct((2 * X, 1, nao), jnp.float32),
        in_specs=[vmem] * (1 + Y),
        out_specs=vmem,
        cost_estimate=pl.CostEstimate(flops=1 << 24, bytes_accessed=3 << 20, transcendentals=0),
        name="transform",
    )(got, *coefs)


def on_device(density, chol_vectors, virt_coef):
    rows, inner = density.shape
    width = chol_vectors.shape[1]
    virt_rows, nao = virt_coef.shape
    here, core, half = lax.axis_index("x"), lax.axis_index("c"), lax.axis_index("zh")
    even = lax.rem(here, 2) == 0
    depth = -(-inner // (2 * BLOCK)) * BLOCK
    pad = 2 * depth - inner
    keep = lax.rem((here + 1) // 2, 2)
    keep, give = keep * depth, (1 - keep) * depth

    vectors = jnp.pad(chol_vectors.T, ((0, 0), (0, pad)))
    mine = lax.dynamic_slice(vectors, (0, keep), (width, depth))
    sent = lax.dynamic_slice(vectors, (0, give), (width, depth))
    got = lax.ppermute(sent, "x", PAIR)
    chunk = jnp.concatenate([jnp.where(even, mine, got), jnp.where(even, got, mine)], axis=0)
    own = ring_gather(chunk)
    cross = [
        lax.ppermute(jnp.concatenate(own[first:last], axis=0), "x", CROSS)
        for first, last in ((0, 3), (3, 5), (5, 7), (7, 8))
    ]

    dens = jnp.pad(density.T, ((0, pad), (0, LANES - rows)))
    kept = lax.dynamic_slice(dens, (keep, 0), (depth, LANES))
    given = lax.dynamic_slice(dens, (give, 0), (depth, LANES))
    other = lax.ppermute(given, "x", PAIR)
    pieces = [kept, swap(kept, "c"), other, swap(other, "c")]

    coef = virt_coef.T
    part = -(-nao // (X * C * 16)) * 16
    coef = jnp.pad(coef, ((0, X * C * part - nao), (0, LANES - virt_rows)))
    far = lax.dynamic_slice(coef, ((here * C + core) * part, 0), (part, LANES))
    far = swap(far, "zh")
    far = gathered(far, ("x", "c"), X * C).reshape(X * C * part, LANES)
    pair = jnp.where(half == core, jnp.stack([coef, far]), jnp.stack([far, coef]))
    coefs = [pair]
    for shift in (1, 3, 2):
        coefs.append(lax.ppermute(pair, "y", [(i, (i + shift) % Y) for i in range(Y)]))

    gamma = contract(own, cross, pieces)
    gamma = exchange(gamma.reshape(X * Y, ZL * ZH * PIECES, LANES), ("x", "y"))
    gamma = regroup(gamma.reshape(X * Y, ZL, ZH * PIECES, LANES))
    gamma = exchange(gamma.reshape(ZH * ZL, 2 * X, LANES), ("zh", "zl"))
    return transform(gamma, coefs, nao)


def solution(mesh):
    split = Mesh(mesh.devices.reshape(X, ZL, C, Y, ZH), AXES)
    return jax.shard_map(
        on_device,
        mesh=split,
        in_specs=(P(("x", "zl", "c"), ("y", "zh")), P(("y", "zh"), ("x", "zl", "c")), P(("y", "zh"), None)),
        out_specs=P(None, AXES, None),
        check_vma=False,
    )
```

```python
import jax
import jax.numpy as jnp
from jax import lax
from jax.experimental import pallas as pl
from jax.experimental.pallas import tpu as pltpu
from jax.sharding import Mesh
from jax.sharding import PartitionSpec as P


AXES = ("x", "zl", "c", "y", "zh")
X, ZL, C, Y, ZH = 4, 8, 2, 4, 2
FOLD = (0, 2, 4, 6, 7, 5, 3, 1)
STEPS = (0, -1, 1, -2, 2, -3, 3, 4)
PAIR = [(0, 1), (1, 0), (2, 3), (3, 2)]
CROSS = [(1, 2), (2, 1), (3, 0), (0, 3)]
LANES = 128
BLOCK = 10 * LANES
PIECES = 4


def fold_ring(step):
    return [(FOLD[i], FOLD[(i + step) % ZL]) for i in range(ZL)]


def swap(shard, axis):
    return lax.ppermute(shard, axis, [(0, 1), (1, 0)])


def exchange(shard, axes):
    return lax.all_to_all(shard, axes, split_axis=0, concat_axis=0, tiled=True)


def ring_gather(piece):
    parts = [piece]
    up, down = piece, piece
    for _ in range(1, ZL // 2):
        up = lax.ppermute(up, "zl", fold_ring(1))
        down = lax.ppermute(down, "zl", fold_ring(-1))
        parts += [up, down]
    return parts + [lax.ppermute(up, "zl", fold_ring(1))]


def ring_source(step):
    here = lax.axis_index("zl")
    place = jnp.where(lax.rem(here, 2) == 0, here // 2, (2 * ZL - 1 - here) // 2)
    place = lax.rem(place + step + ZL, ZL)
    return jnp.where(place < ZL // 2, 2 * place, 2 * ZL - 1 - 2 * place)


def contract_kernel(*refs):
    own, cross, (a, b, c, d, out, acc) = refs[:ZL], refs[ZL : ZL + 4], refs[ZL + 4 :]
    index = pl.program_id(0)
    here = lax.axis_index("x")

    @pl.when(index == 0)
    def _():
        acc[...] = jnp.zeros_like(acc)

    own = jnp.concatenate([part[...] for part in own], axis=0)
    cross = jnp.concatenate([part[...] for part in cross], axis=0)
    low = here < X // 2
    left = jnp.concatenate([jnp.where(low, own, cross), jnp.where(low, cross, own)], axis=0)
    even = lax.rem(here, 2) == 0
    one = jnp.concatenate([a[...], b[...]], axis=1)
    two = jnp.concatenate([c[...], d[...]], axis=1)
    for slot, right in enumerate((jnp.where(even, one, two), jnp.where(even, two, one))):
        both = jnp.dot(left, right, preferred_element_type=jnp.float32)
        acc[2 * slot] += both[:, :LANES]
        acc[2 * slot + 1] += both[:, LANES:]

    @pl.when(index == pl.num_programs(0) - 1)
    def _():
        for piece in range(PIECES):
            for half in range(2):
                for slot in range(ZL):
                    for owner in range(ZH):
                        got = acc[piece, pl.ds((half * ZL + slot) * 16 + owner, 8, stride=2), :]
                        start = half * 512 + (slot * ZH + owner) * PIECES + piece
                        out[pl.ds(start, 8, stride=ZL * ZH * PIECES), :] = got


def contract(own, cross, pieces):
    inner = own[0].shape[1]
    columns = X * ZL * own[0].shape[0] // 2
    lefts = [pl.BlockSpec((part.shape[0], BLOCK), lambda k: (0, k)) for part in own + cross]
    rights = [pl.BlockSpec((BLOCK, LANES), lambda k: (k, 0))] * len(pieces)
    return pl.pallas_call(
        contract_kernel,
        grid=(inner // BLOCK,),
        out_shape=jax.ShapeDtypeStruct((columns * PIECES, LANES), jnp.float32),
        in_specs=lefts + rights,
        out_specs=pl.BlockSpec((columns * PIECES, LANES), lambda k: (0, 0)),
        scratch_shapes=[pltpu.VMEM((PIECES, columns, LANES), jnp.float32)],
        cost_estimate=pl.CostEstimate(
            flops=2 * columns * inner * PIECES * LANES, bytes_accessed=10 << 20, transcendentals=0
        ),
        name="contract",
    )(*own, *cross, *pieces)


def regroup_kernel(got, out):
    for slot in range(ZL):
        target = ring_source(STEPS[slot])
        for pair in range(2):
            total = got[pair * 2 * Y, slot]
            for source in range(pair * 2 * Y + 1, (pair + 1) * 2 * Y):
                total += got[source, slot]
            for owner in range(ZH):
                out[owner, target, pair * PIECES : (pair + 1) * PIECES, :] = total[
                    owner * PIECES : (owner + 1) * PIECES
                ]


def regroup(got):
    vmem = pl.BlockSpec(memory_space=pltpu.VMEM)
    return pl.pallas_call(
        regroup_kernel,
        in_specs=[vmem],
        out_specs=vmem,
        out_shape=jax.ShapeDtypeStruct((ZH, ZL, 2 * X, LANES), jnp.float32),
        cost_estimate=pl.CostEstimate(flops=1 << 17, bytes_accessed=1 << 19, transcendentals=0),
        compiler_params=pltpu.CompilerParams(vmem_limit_bytes=8 << 20),
        name="regroup",
    )(got)


def transform_kernel(got, near, other, out):
    nao = out.shape[2]
    here, core = lax.axis_index("y"), lax.axis_index("c")
    totals = [[0.0, 0.0], [0.0, 0.0]]
    for slot, shift in enumerate((0, 1, 3, 2)):
        block = lax.rem(here - shift + Y, Y)
        tiles = [got[Y * h + block] + got[ZL + Y * h + block] for h in range(2)]
        rest = jnp.concatenate(tiles, axis=0)
        terms = []
        for _ in range(3):
            terms.append(rest.astype(jnp.bfloat16))
            rest = rest - terms[-1].astype(jnp.float32)
        terms = jnp.concatenate(terms, axis=0)
        for side in range(2):
            source = core if side == 0 else 1 - core
            for index, coef in enumerate((near, other)):
                got_part = lax.dot_general(
                    terms, coef[slot, source], (((1,), (1,)), ((), ())), preferred_element_type=jnp.float32
                )
                totals[index][side] += (got_part[:16] + got_part[16:32]) + got_part[32:]
    first = core == 0
    both = []
    for side in range(2):
        low = jnp.where(first, totals[0][side], totals[1][side])
        high = jnp.where(first, totals[1][side], totals[0][side])
        both.append(jnp.concatenate([low, high], axis=1))
    for source in range(X):
        for h in range(2):
            row = h * 2 * X + 2 * source
            out[2 * source + h] = (both[0][row : row + 1] + both[1][row + 1 : row + 2])[:, :nao]


def transform(got, near, other, nao):
    vmem = pl.BlockSpec(memory_space=pltpu.VMEM)
    return pl.pallas_call(
        transform_kernel,
        out_shape=jax.ShapeDtypeStruct((2 * X, 1, nao), jnp.float32),
        in_specs=[vmem] * 3,
        out_specs=vmem,
        cost_estimate=pl.CostEstimate(flops=1 << 24, bytes_accessed=3 << 20, transcendentals=0),
        compiler_params=pltpu.CompilerParams(vmem_limit_bytes=16 << 20),
        name="transform",
    )(got, near, other)


def on_device(density, chol_vectors, virt_coef):
    rows, inner = density.shape
    width = chol_vectors.shape[1]
    virt_rows, nao = virt_coef.shape
    here, core, half = lax.axis_index("x"), lax.axis_index("c"), lax.axis_index("zh")
    even = lax.rem(here, 2) == 0
    depth = -(-inner // (2 * BLOCK)) * BLOCK
    pad = 2 * depth - inner
    keep = lax.rem((here + 1) // 2, 2)
    keep, give = keep * depth, (1 - keep) * depth

    vectors = jnp.pad(chol_vectors.T, ((0, 0), (0, pad)))
    mine = lax.dynamic_slice(vectors, (0, keep), (width, depth))
    sent = lax.dynamic_slice(vectors, (0, give), (width, depth))
    got = lax.ppermute(sent, "x", PAIR)
    chunk = jnp.concatenate([jnp.where(even, mine, got), jnp.where(even, got, mine)], axis=0)
    own = ring_gather(chunk)
    cross = [
        lax.ppermute(jnp.concatenate(own[first:last], axis=0), "x", CROSS)
        for first, last in ((0, 3), (3, 5), (5, 7), (7, 8))
    ]

    dens = jnp.pad(density.T, ((0, pad), (0, LANES - rows)))
    kept = lax.dynamic_slice(dens, (keep, 0), (depth, LANES))
    given = lax.dynamic_slice(dens, (give, 0), (depth, LANES))
    other = lax.ppermute(given, "x", PAIR)
    pieces = [kept, swap(kept, "c"), other, swap(other, "c")]

    part = -(-nao // (C * LANES)) * LANES
    coef = jnp.pad(virt_coef.T, ((0, C * part - nao), (0, LANES - virt_rows)))
    mine = lax.dynamic_slice(coef, (core * part, 0), (part, LANES))
    far = swap(mine, "zh")
    pair = jnp.where(half == 0, jnp.stack([mine, far]), jnp.stack([far, mine]))
    coefs = [pair]
    for shift in (1, 3, 2):
        coefs.append(lax.ppermute(pair, "y", [(i, (i + shift) % Y) for i in range(Y)]))
    coefs = jnp.stack(coefs)
    coefs = [coefs, swap(coefs, "c")]

    gamma = contract(own, cross, pieces)
    gamma = exchange(gamma.reshape(X * Y, ZL * ZH * PIECES, LANES), ("x", "y"))
    gamma = regroup(gamma.reshape(X * Y, ZL, ZH * PIECES, LANES))
    gamma = exchange(gamma.reshape(ZH * ZL, 2 * X, LANES), ("zh", "zl"))
    return transform(gamma, *coefs, nao)


def solution(mesh):
    split = Mesh(mesh.devices.reshape(X, ZL, C, Y, ZH), AXES)
    return jax.shard_map(
        on_device,
        mesh=split,
        in_specs=(P(("x", "zl", "c"), ("y", "zh")), P(("y", "zh"), ("x", "zl", "c")), P(("y", "zh"), None)),
        out_specs=P(None, AXES, None),
        check_vma=False,
    )
```

```python
import jax
import jax.numpy as jnp
from jax import lax
from jax.experimental import pallas as pl
from jax.experimental.pallas import tpu as pltpu
from jax.sharding import Mesh
from jax.sharding import PartitionSpec as P


AXES = ("x", "zl", "c", "y", "zh")
X, ZL, C, Y, ZH = 4, 8, 2, 4, 2
FOLD = (0, 2, 4, 6, 7, 5, 3, 1)
STEPS = (0, -1, 1, -2, 2, -3, 3, 4)
PAIR = [(0, 1), (1, 0), (2, 3), (3, 2)]
CROSS = [(1, 2), (2, 1), (3, 0), (0, 3)]
LANES = 128
BLOCK = 10 * LANES
PIECES = 4


def fold_ring(step):
    return [(FOLD[i], FOLD[(i + step) % ZL]) for i in range(ZL)]


def swap(shard, axis):
    return lax.ppermute(shard, axis, [(0, 1), (1, 0)])


def exchange(shard, axes):
    return lax.all_to_all(shard, axes, split_axis=0, concat_axis=0, tiled=True)


def ring_gather(piece):
    parts = [piece]
    up, down = piece, piece
    for _ in range(1, ZL // 2):
        up = lax.ppermute(up, "zl", fold_ring(1))
        down = lax.ppermute(down, "zl", fold_ring(-1))
        parts += [up, down]
    return parts + [lax.ppermute(up, "zl", fold_ring(1))]


def ring_source(step):
    here = lax.axis_index("zl")
    place = jnp.where(lax.rem(here, 2) == 0, here // 2, (2 * ZL - 1 - here) // 2)
    place = lax.rem(place + step + ZL, ZL)
    return jnp.where(place < ZL // 2, 2 * place, 2 * ZL - 1 - 2 * place)


def contract_kernel(*refs):
    own, cross, (a, b, c, d, out, acc) = refs[:ZL], refs[ZL : ZL + 4], refs[ZL + 4 :]
    index = pl.program_id(0)
    here = lax.axis_index("x")

    @pl.when(index == 0)
    def _():
        acc[...] = jnp.zeros_like(acc)

    own = jnp.concatenate([part[...] for part in own], axis=0)
    cross = jnp.concatenate([part[...] for part in cross], axis=0)
    low = here < X // 2
    left = jnp.concatenate([jnp.where(low, own, cross), jnp.where(low, cross, own)], axis=0)
    even = lax.rem(here, 2) == 0
    one = jnp.concatenate([a[...], b[...]], axis=1)
    two = jnp.concatenate([c[...], d[...]], axis=1)
    for slot, right in enumerate((jnp.where(even, one, two), jnp.where(even, two, one))):
        both = jnp.dot(left, right, preferred_element_type=jnp.float32)
        acc[2 * slot] += both[:, :LANES]
        acc[2 * slot + 1] += both[:, LANES:]

    @pl.when(index == pl.num_programs(0) - 1)
    def _():
        for piece in range(PIECES):
            for half in range(2):
                for slot in range(ZL):
                    for owner in range(ZH):
                        got = acc[piece, pl.ds((half * ZL + slot) * 16 + owner, 8, stride=2), :]
                        start = half * 512 + (slot * ZH + owner) * PIECES + piece
                        out[pl.ds(start, 8, stride=ZL * ZH * PIECES), :] = got


def contract(own, cross, pieces):
    inner = own[0].shape[1]
    columns = X * ZL * own[0].shape[0] // 2
    lefts = [pl.BlockSpec((part.shape[0], BLOCK), lambda k: (0, k)) for part in own + cross]
    rights = [pl.BlockSpec((BLOCK, LANES), lambda k: (k, 0))] * len(pieces)
    return pl.pallas_call(
        contract_kernel,
        grid=(inner // BLOCK,),
        out_shape=jax.ShapeDtypeStruct((columns * PIECES, LANES), jnp.float32),
        in_specs=lefts + rights,
        out_specs=pl.BlockSpec((columns * PIECES, LANES), lambda k: (0, 0)),
        scratch_shapes=[pltpu.VMEM((PIECES, columns, LANES), jnp.float32)],
        cost_estimate=pl.CostEstimate(
            flops=2 * columns * inner * PIECES * LANES, bytes_accessed=10 << 20, transcendentals=0
        ),
        name="contract",
    )(*own, *cross, *pieces)


def regroup_kernel(got, out):
    for slot in range(ZL):
        target = ring_source(STEPS[slot])
        for pair in range(2):
            total = got[pair * 2 * Y, slot]
            for source in range(pair * 2 * Y + 1, (pair + 1) * 2 * Y):
                total += got[source, slot]
            for owner in range(ZH):
                out[owner, target, pair * PIECES : (pair + 1) * PIECES, :] = total[
                    owner * PIECES : (owner + 1) * PIECES
                ]


def regroup(got):
    vmem = pl.BlockSpec(memory_space=pltpu.VMEM)
    return pl.pallas_call(
        regroup_kernel,
        in_specs=[vmem],
        out_specs=vmem,
        out_shape=jax.ShapeDtypeStruct((ZH, ZL, 2 * X, LANES), jnp.float32),
        cost_estimate=pl.CostEstimate(flops=1 << 17, bytes_accessed=1 << 19, transcendentals=0),
        compiler_params=pltpu.CompilerParams(vmem_limit_bytes=8 << 20),
        name="regroup",
    )(got)


def transform_kernel(got, near, other, out):
    nao = out.shape[2]
    core = lax.axis_index("c")
    source = jnp.where(core == lax.axis_index("zh"), 0, 1)
    totals = [[0.0, 0.0], [0.0, 0.0]]
    for block in range(Y):
        tiles = [got[Y * h + block] + got[ZL + Y * h + block] for h in range(2)]
        rest = jnp.concatenate(tiles, axis=0)
        terms = []
        for _ in range(3):
            terms.append(rest.astype(jnp.bfloat16))
            rest = rest - terms[-1].astype(jnp.float32)
        terms = jnp.concatenate(terms, axis=0)
        for side in range(2):
            for index, coef in enumerate((near, other)):
                got_part = lax.dot_general(
                    terms, coef[block, source if side == 0 else 1 - source], (((1,), (1,)), ((), ())), preferred_element_type=jnp.float32
                )
                totals[index][side] += (got_part[:16] + got_part[16:32]) + got_part[32:]
    first = core == 0
    both = []
    for side in range(2):
        low = jnp.where(first, totals[0][side], totals[1][side])
        high = jnp.where(first, totals[1][side], totals[0][side])
        both.append(jnp.concatenate([low, high], axis=1))
    for source in range(X):
        for h in range(2):
            row = h * 2 * X + 2 * source
            out[2 * source + h] = (both[0][row : row + 1] + both[1][row + 1 : row + 2])[:, :nao]


def transform(got, near, other, nao):
    vmem = pl.BlockSpec(memory_space=pltpu.VMEM)
    return pl.pallas_call(
        transform_kernel,
        out_shape=jax.ShapeDtypeStruct((2 * X, 1, nao), jnp.float32),
        in_specs=[vmem] * 3,
        out_specs=vmem,
        cost_estimate=pl.CostEstimate(flops=1 << 24, bytes_accessed=3 << 20, transcendentals=0),
        compiler_params=pltpu.CompilerParams(vmem_limit_bytes=16 << 20),
        name="transform",
    )(got, near, other)


def on_device(density, chol_vectors, virt_coef):
    rows, inner = density.shape
    width = chol_vectors.shape[1]
    virt_rows, nao = virt_coef.shape
    here, core = lax.axis_index("x"), lax.axis_index("c")
    even = lax.rem(here, 2) == 0
    depth = -(-inner // (2 * BLOCK)) * BLOCK
    pad = 2 * depth - inner
    keep = lax.rem((here + 1) // 2, 2)
    keep, give = keep * depth, (1 - keep) * depth

    vectors = jnp.pad(chol_vectors.T, ((0, 0), (0, pad)))
    mine = lax.dynamic_slice(vectors, (0, keep), (width, depth))
    sent = lax.dynamic_slice(vectors, (0, give), (width, depth))
    got = lax.ppermute(sent, "x", PAIR)
    chunk = jnp.concatenate([jnp.where(even, mine, got), jnp.where(even, got, mine)], axis=0)
    own = ring_gather(chunk)
    cross = [
        lax.ppermute(jnp.concatenate(own[first:last], axis=0), "x", CROSS)
        for first, last in ((0, 3), (3, 5), (5, 7), (7, 8))
    ]

    dens = jnp.pad(density.T, ((0, pad), (0, LANES - rows)))
    kept = lax.dynamic_slice(dens, (keep, 0), (depth, LANES))
    given = lax.dynamic_slice(dens, (give, 0), (depth, LANES))
    other = lax.ppermute(given, "x", PAIR)
    pieces = [kept, swap(kept, "c"), other, swap(other, "c")]

    part = -(-nao // (C * LANES)) * LANES
    coef = jnp.pad(virt_coef.T, ((0, C * part - nao), (0, LANES - virt_rows)))
    mine = lax.dynamic_slice(coef, (core * part, 0), (part, LANES))
    far = swap(mine, "zh")
    pair = jnp.broadcast_to(jnp.stack([mine, far])[None], (Y, ZH, part, LANES))
    coefs = exchange(pair, "y")
    coefs = [coefs.reshape(Y, ZH, part, LANES), swap(coefs, "c").reshape(Y, ZH, part, LANES)]

    gamma = contract(own, cross, pieces)
    gamma = exchange(gamma.reshape(X * Y, ZL * ZH * PIECES, LANES), ("x", "y"))
    gamma = regroup(gamma.reshape(X * Y, ZL, ZH * PIECES, LANES))
    gamma = exchange(gamma.reshape(ZH * ZL, 2 * X, LANES), ("zh", "zl"))
    return transform(gamma, *coefs, nao)


def solution(mesh):
    split = Mesh(mesh.devices.reshape(X, ZL, C, Y, ZH), AXES)
    return jax.shard_map(
        on_device,
        mesh=split,
        in_specs=(P(("x", "zl", "c"), ("y", "zh")), P(("y", "zh"), ("x", "zl", "c")), P(("y", "zh"), None)),
        out_specs=P(None, AXES, None),
        check_vma=False,
    )
```

```python
import jax
import jax.numpy as jnp
from jax import lax
from jax.experimental import pallas as pl
from jax.experimental.pallas import tpu as pltpu
from jax.sharding import Mesh
from jax.sharding import PartitionSpec as P


AXES = ("x", "zl", "c", "y", "zh")
X, ZL, C, Y, ZH = 4, 8, 2, 4, 2
FOLD = (0, 2, 4, 6, 7, 5, 3, 1)
STEPS = (0, -1, 1, -2, 2, -3, 3, 4)
PAIR = [(0, 1), (1, 0), (2, 3), (3, 2)]
CROSS = [(1, 2), (2, 1), (3, 0), (0, 3)]
LANES = 128
BLOCK = 25 * LANES
PIECES = 4


def fold_ring(step):
    return [(FOLD[i], FOLD[(i + step) % ZL]) for i in range(ZL)]


def swap(shard, axis):
    return lax.ppermute(shard, axis, [(0, 1), (1, 0)])


def exchange(shard, axes):
    return lax.all_to_all(shard, axes, split_axis=0, concat_axis=0, tiled=True)


def ring_gather(piece):
    parts = [piece]
    up, down = piece, piece
    for _ in range(1, ZL // 2):
        up = lax.ppermute(up, "zl", fold_ring(1))
        down = lax.ppermute(down, "zl", fold_ring(-1))
        parts += [up, down]
    return parts + [lax.ppermute(up, "zl", fold_ring(1))]


def ring_source(step):
    here = lax.axis_index("zl")
    place = jnp.where(lax.rem(here, 2) == 0, here // 2, (2 * ZL - 1 - here) // 2)
    place = lax.rem(place + step + ZL, ZL)
    return jnp.where(place < ZL // 2, 2 * place, 2 * ZL - 1 - 2 * place)


def contract_kernel(*refs):
    own, cross, (a, b, c, d, out, acc) = refs[:ZL], refs[ZL : ZL + 4], refs[ZL + 4 :]
    index = pl.program_id(0)
    here = lax.axis_index("x")

    @pl.when(index == 0)
    def _():
        acc[...] = jnp.zeros_like(acc)

    own = jnp.concatenate([part[...] for part in own], axis=0)
    cross = jnp.concatenate([part[...] for part in cross], axis=0)
    low = here < X // 2
    left = jnp.concatenate([jnp.where(low, own, cross), jnp.where(low, cross, own)], axis=0)
    even = lax.rem(here, 2) == 0
    one = jnp.concatenate([a[...], b[...]], axis=1)
    two = jnp.concatenate([c[...], d[...]], axis=1)
    for slot, right in enumerate((jnp.where(even, one, two), jnp.where(even, two, one))):
        both = jnp.dot(left, right, preferred_element_type=jnp.float32)
        acc[2 * slot] += both[:, :LANES]
        acc[2 * slot + 1] += both[:, LANES:]

    @pl.when(index == pl.num_programs(0) - 1)
    def _():
        for piece in range(PIECES):
            for half in range(2):
                for slot in range(ZL):
                    for owner in range(ZH):
                        got = acc[piece, pl.ds((half * ZL + slot) * 16 + owner, 8, stride=2), :]
                        start = half * 512 + (slot * ZH + owner) * PIECES + piece
                        out[pl.ds(start, 8, stride=ZL * ZH * PIECES), :] = got


def contract(own, cross, pieces):
    inner = own[0].shape[1]
    columns = X * ZL * own[0].shape[0] // 2
    lefts = [pl.BlockSpec((part.shape[0], BLOCK), lambda k: (0, k)) for part in own + cross]
    rights = [pl.BlockSpec((BLOCK, LANES), lambda k: (k, 0))] * len(pieces)
    return pl.pallas_call(
        contract_kernel,
        grid=(inner // BLOCK,),
        out_shape=jax.ShapeDtypeStruct((columns * PIECES, LANES), jnp.float32),
        in_specs=lefts + rights,
        out_specs=pl.BlockSpec((columns * PIECES, LANES), lambda k: (0, 0)),
        scratch_shapes=[pltpu.VMEM((PIECES, columns, LANES), jnp.float32)],
        cost_estimate=pl.CostEstimate(
            flops=2 * columns * inner * PIECES * LANES, bytes_accessed=10 << 20, transcendentals=0
        ),
        name="contract",
    )(*own, *cross, *pieces)


def regroup_kernel(got, out):
    for slot in range(ZL):
        target = ring_source(STEPS[slot])
        for pair in range(2):
            total = got[pair * 2 * Y, slot]
            for source in range(pair * 2 * Y + 1, (pair + 1) * 2 * Y):
                total += got[source, slot]
            for owner in range(ZH):
                out[owner, target, pair * PIECES : (pair + 1) * PIECES, :] = total[
                    owner * PIECES : (owner + 1) * PIECES
                ]


def regroup(got):
    vmem = pl.BlockSpec(memory_space=pltpu.VMEM)
    return pl.pallas_call(
        regroup_kernel,
        in_specs=[vmem],
        out_specs=vmem,
        out_shape=jax.ShapeDtypeStruct((ZH, ZL, 2 * X, LANES), jnp.float32),
        cost_estimate=pl.CostEstimate(flops=1 << 17, bytes_accessed=1 << 19, transcendentals=0),
        compiler_params=pltpu.CompilerParams(vmem_limit_bytes=8 << 20),
        name="regroup",
    )(got)


def transform_kernel(got, near, other, out):
    nao = out.shape[2]
    core = lax.axis_index("c")
    source = jnp.where(core == lax.axis_index("zh"), 0, 1)
    totals = [[0.0, 0.0], [0.0, 0.0]]
    for block in range(Y):
        tiles = [got[Y * h + block] + got[ZL + Y * h + block] for h in range(2)]
        rest = jnp.concatenate(tiles, axis=0)
        terms = []
        for _ in range(3):
            terms.append(rest.astype(jnp.bfloat16))
            rest = rest - terms[-1].astype(jnp.float32)
        terms = jnp.concatenate(terms, axis=0)
        for side in range(2):
            for index, coef in enumerate((near, other)):
                got_part = lax.dot_general(
                    terms, coef[block, source if side == 0 else 1 - source], (((1,), (1,)), ((), ())), preferred_element_type=jnp.float32
                )
                totals[index][side] += (got_part[:16] + got_part[16:32]) + got_part[32:]
    first = core == 0
    both = []
    for side in range(2):
        low = jnp.where(first, totals[0][side], totals[1][side])
        high = jnp.where(first, totals[1][side], totals[0][side])
        both.append(jnp.concatenate([low, high], axis=1))
    for source in range(X):
        for h in range(2):
            row = h * 2 * X + 2 * source
            out[2 * source + h] = (both[0][row : row + 1] + both[1][row + 1 : row + 2])[:, :nao]


def transform(got, near, other, nao):
    vmem = pl.BlockSpec(memory_space=pltpu.VMEM)
    return pl.pallas_call(
        transform_kernel,
        out_shape=jax.ShapeDtypeStruct((2 * X, 1, nao), jnp.float32),
        in_specs=[vmem] * 3,
        out_specs=vmem,
        cost_estimate=pl.CostEstimate(flops=1 << 24, bytes_accessed=3 << 20, transcendentals=0),
        compiler_params=pltpu.CompilerParams(vmem_limit_bytes=16 << 20),
        name="transform",
    )(got, near, other)


def on_device(density, chol_vectors, virt_coef):
    rows, inner = density.shape
    width = chol_vectors.shape[1]
    virt_rows, nao = virt_coef.shape
    here, core = lax.axis_index("x"), lax.axis_index("c")
    even = lax.rem(here, 2) == 0
    depth = -(-inner // (2 * BLOCK)) * BLOCK
    pad = 2 * depth - inner
    keep = lax.rem((here + 1) // 2, 2)
    keep, give = keep * depth, (1 - keep) * depth

    vectors = jnp.pad(chol_vectors.T, ((0, 0), (0, pad)))
    mine = lax.dynamic_slice(vectors, (0, keep), (width, depth))
    sent = lax.dynamic_slice(vectors, (0, give), (width, depth))
    got = lax.ppermute(sent, "x", PAIR)
    chunk = jnp.concatenate([jnp.where(even, mine, got), jnp.where(even, got, mine)], axis=0)
    own = ring_gather(chunk)
    cross = [
        lax.ppermute(jnp.concatenate(own[first:last], axis=0), "x", CROSS)
        for first, last in ((0, 3), (3, 5), (5, 7), (7, 8))
    ]

    dens = jnp.pad(density.T, ((0, pad), (0, LANES - rows)))
    kept = lax.dynamic_slice(dens, (keep, 0), (depth, LANES))
    given = lax.dynamic_slice(dens, (give, 0), (depth, LANES))
    other = lax.ppermute(given, "x", PAIR)
    pieces = [kept, swap(kept, "c"), other, swap(other, "c")]

    part = -(-nao // (C * LANES)) * LANES
    coef = jnp.pad(virt_coef.T, ((0, C * part - nao), (0, LANES - virt_rows)))
    mine = lax.dynamic_slice(coef, (core * part, 0), (part, LANES))
    mirror = [(z * ZH + h, (ZL - 1 - z) * ZH + 1 - h) for z in range(ZL) for h in range(ZH)]
    far = lax.ppermute(mine, ("zl", "zh"), mirror)
    pair = jnp.broadcast_to(jnp.stack([mine, far])[None], (Y, ZH, part, LANES))
    coefs = exchange(pair, "y")
    coefs = [coefs.reshape(Y, ZH, part, LANES), swap(coefs, "c").reshape(Y, ZH, part, LANES)]

    gamma = contract(own, cross, pieces)
    gamma = exchange(gamma.reshape(X * Y, ZL * ZH * PIECES, LANES), ("x", "y"))
    gamma = regroup(gamma.reshape(X * Y, ZL, ZH * PIECES, LANES))
    gamma = exchange(gamma.reshape(ZH * ZL, 2 * X, LANES), ("zh", "zl"))
    return transform(gamma, *coefs, nao)


def solution(mesh):
    split = Mesh(mesh.devices.reshape(X, ZL, C, Y, ZH), AXES)
    return jax.shard_map(
        on_device,
        mesh=split,
        in_specs=(P(("x", "zl", "c"), ("y", "zh")), P(("y", "zh"), ("x", "zl", "c")), P(("y", "zh"), None)),
        out_specs=P(None, AXES, None),
        check_vma=False,
    )
```

```python
import jax
import jax.numpy as jnp
from jax import lax
from jax.experimental import pallas as pl
from jax.experimental.pallas import tpu as pltpu
from jax.sharding import Mesh
from jax.sharding import PartitionSpec as P


AXES = ("x", "zl", "c", "y", "zh")
X, ZL, C, Y, ZH = 4, 8, 2, 4, 2
FOLD = (0, 2, 4, 6, 7, 5, 3, 1)
STEPS = (0, -1, 1, -2, 2, -3, 3, 4)
PAIR = [(0, 1), (1, 0), (2, 3), (3, 2)]
CROSS = [(1, 2), (2, 1), (3, 0), (0, 3)]
LANES = 128
BLOCK = 25 * LANES
PIECES = 4


def fold_ring(step):
    return [(FOLD[i], FOLD[(i + step) % ZL]) for i in range(ZL)]


def swap(shard, axis):
    return lax.ppermute(shard, axis, [(0, 1), (1, 0)])


def exchange(shard, axes):
    return lax.all_to_all(shard, axes, split_axis=0, concat_axis=0, tiled=True)


def ring_gather(piece):
    parts = [piece]
    up, down = piece, piece
    for _ in range(1, ZL // 2):
        up = lax.ppermute(up, "zl", fold_ring(1))
        down = lax.ppermute(down, "zl", fold_ring(-1))
        parts += [up, down]
    return parts + [lax.ppermute(up, "zl", fold_ring(1))]


def ring_source(step):
    here = lax.axis_index("zl")
    place = jnp.where(lax.rem(here, 2) == 0, here // 2, (2 * ZL - 1 - here) // 2)
    place = lax.rem(place + step + ZL, ZL)
    return jnp.where(place < ZL // 2, 2 * place, 2 * ZL - 1 - 2 * place)


def contract_kernel(*refs):
    own, cross, (a, b, c, d, out, acc) = refs[:ZL], refs[ZL : ZL + 4], refs[ZL + 4 :]
    index = pl.program_id(0)
    here = lax.axis_index("x")

    @pl.when(index == 0)
    def _():
        acc[...] = jnp.zeros_like(acc)

    own = jnp.concatenate([part[...] for part in own], axis=0)
    cross = jnp.concatenate([part[...] for part in cross], axis=0)
    low = here < X // 2
    left = jnp.concatenate([jnp.where(low, own, cross), jnp.where(low, cross, own)], axis=0)
    even = lax.rem(here, 2) == 0
    one = jnp.concatenate([a[...], b[...]], axis=1)
    two = jnp.concatenate([c[...], d[...]], axis=1)
    for slot, right in enumerate((jnp.where(even, one, two), jnp.where(even, two, one))):
        both = jnp.dot(left, right, preferred_element_type=jnp.float32)
        acc[2 * slot] += both[:, :LANES]
        acc[2 * slot + 1] += both[:, LANES:]

    @pl.when(index == pl.num_programs(0) - 1)
    def _():
        for piece in range(PIECES):
            for half in range(2):
                for slot in range(ZL):
                    for owner in range(ZH):
                        got = acc[piece, pl.ds((half * ZL + slot) * 16 + owner, 8, stride=2), :]
                        start = half * 512 + (slot * ZH + owner) * PIECES + piece
                        out[pl.ds(start, 8, stride=ZL * ZH * PIECES), :] = got


def contract(own, cross, pieces):
    inner = own[0].shape[1]
    columns = X * ZL * own[0].shape[0] // 2
    lefts = [pl.BlockSpec((part.shape[0], BLOCK), lambda k: (0, k)) for part in own + cross]
    rights = [pl.BlockSpec((BLOCK, LANES), lambda k: (k, 0))] * len(pieces)
    return pl.pallas_call(
        contract_kernel,
        grid=(inner // BLOCK,),
        out_shape=jax.ShapeDtypeStruct((columns * PIECES, LANES), jnp.float32),
        in_specs=lefts + rights,
        out_specs=pl.BlockSpec((columns * PIECES, LANES), lambda k: (0, 0)),
        scratch_shapes=[pltpu.VMEM((PIECES, columns, LANES), jnp.float32)],
        cost_estimate=pl.CostEstimate(
            flops=2 * columns * inner * PIECES * LANES, bytes_accessed=10 << 20, transcendentals=0
        ),
        name="contract",
    )(*own, *cross, *pieces)


def regroup_kernel(got, out):
    for slot in range(ZL):
        target = ring_source(STEPS[slot])
        for pair in range(2):
            total = got[pair * 2 * Y, slot]
            for source in range(pair * 2 * Y + 1, (pair + 1) * 2 * Y):
                total += got[source, slot]
            for owner in range(ZH):
                out[owner, target, pair * PIECES : (pair + 1) * PIECES, :] = total[
                    owner * PIECES : (owner + 1) * PIECES
                ]


def regroup(got):
    vmem = pl.BlockSpec(memory_space=pltpu.VMEM)
    return pl.pallas_call(
        regroup_kernel,
        in_specs=[vmem],
        out_specs=vmem,
        out_shape=jax.ShapeDtypeStruct((ZH, ZL, 2 * X, LANES), jnp.float32),
        cost_estimate=pl.CostEstimate(flops=1 << 17, bytes_accessed=1 << 19, transcendentals=0),
        compiler_params=pltpu.CompilerParams(vmem_limit_bytes=8 << 20),
        name="regroup",
    )(got)


def transform_kernel(got, near, other, out):
    nao = out.shape[2]
    part = near.shape[1] // 4
    core, odd = lax.axis_index("c"), lax.rem(lax.axis_index("x"), 2)
    totals = [[[0.0, 0.0] for _ in range(2)] for _ in range(C)]
    for block in range(Y):
        tiles = [got[Y * h + block] + got[ZL + Y * h + block] for h in range(2)]
        rest = jnp.concatenate(tiles, axis=0)
        terms = []
        for _ in range(3):
            terms.append(rest.astype(jnp.bfloat16))
            rest = rest - terms[-1].astype(jnp.float32)
        terms = jnp.concatenate(terms, axis=0)
        for side in range(2):
            local = (core == lax.axis_index("zh")) == (side == 0)
            for index, coef in enumerate((near, other)):
                for quarter in range(2):
                    away = 2 + (odd if quarter == 0 else 1 - odd)
                    start = pl.multiple_of(jnp.where(local, quarter, away) * part, 16)
                    product = lax.dot_general(
                        terms,
                        coef[block, pl.ds(start, part), :],
                        (((1,), (1,)), ((), ())),
                        preferred_element_type=jnp.float32,
                    )
                    totals[index][side][quarter] += (product[:16] + product[16:32]) + product[32:]
    both = []
    for side in range(2):
        halves = [jnp.concatenate(totals[index][side], axis=1) for index in range(C)]
        low = jnp.where(core == 0, halves[0], halves[1])
        high = jnp.where(core == 0, halves[1], halves[0])
        both.append(jnp.concatenate([low, high], axis=1))
    for source in range(X):
        for h in range(2):
            row = h * 2 * X + 2 * source
            out[2 * source + h] = (both[0][row : row + 1] + both[1][row + 1 : row + 2])[:, :nao]


def transform(got, near, other, nao):
    vmem = pl.BlockSpec(memory_space=pltpu.VMEM)
    return pl.pallas_call(
        transform_kernel,
        out_shape=jax.ShapeDtypeStruct((2 * X, 1, nao), jnp.float32),
        in_specs=[vmem] * 3,
        out_specs=vmem,
        cost_estimate=pl.CostEstimate(flops=1 << 24, bytes_accessed=3 << 20, transcendentals=0),
        compiler_params=pltpu.CompilerParams(vmem_limit_bytes=16 << 20),
        name="transform",
    )(got, near, other)


def on_device(density, chol_vectors, virt_coef):
    rows, inner = density.shape
    width = chol_vectors.shape[1]
    virt_rows, nao = virt_coef.shape
    here, core = lax.axis_index("x"), lax.axis_index("c")
    even = lax.rem(here, 2) == 0
    depth = -(-inner // (2 * BLOCK)) * BLOCK
    pad = 2 * depth - inner
    keep = lax.rem((here + 1) // 2, 2)
    keep, give = keep * depth, (1 - keep) * depth

    vectors = jnp.pad(chol_vectors.T, ((0, 0), (0, pad)))
    mine = lax.dynamic_slice(vectors, (0, keep), (width, depth))
    sent = lax.dynamic_slice(vectors, (0, give), (width, depth))
    got = lax.ppermute(sent, "x", PAIR)
    chunk = jnp.concatenate([jnp.where(even, mine, got), jnp.where(even, got, mine)], axis=0)
    own = ring_gather(chunk)
    cross = []
    for first, last in ((0, 3), (3, 5), (5, 7), (7, 8)):
        joined = jnp.concatenate(own[first:last], axis=0)
        cross.append(lax.ppermute(joined, "x", CROSS))

    dens = jnp.pad(density.T, ((0, pad), (0, LANES - rows)))
    kept = lax.dynamic_slice(dens, (keep, 0), (depth, LANES))
    given = lax.dynamic_slice(dens, (give, 0), (depth, LANES))
    other = lax.ppermute(given, "x", PAIR)
    pieces = [kept, swap(kept, "c"), other, swap(other, "c")]

    part = -(-nao // (2 * C * 16)) * 16
    coef = jnp.pad(virt_coef.T, ((0, 2 * C * part - nao), (0, LANES - virt_rows)))
    mine = lax.dynamic_slice(coef, (2 * core * part, 0), (2 * part, LANES))
    quarter = lax.dynamic_slice(coef, ((2 * core + lax.rem(here, 2)) * part, 0), (part, LANES))
    mirror = [(z * ZH + h, (ZL - 1 - z) * ZH + 1 - h) for z in range(ZL) for h in range(ZH)]
    far = lax.ppermute(quarter, ("zl", "zh"), mirror)
    rest = lax.ppermute(far, "x", PAIR)
    pair = jnp.concatenate([mine, far, rest], axis=0)
    pair = jnp.broadcast_to(pair[None], (Y,) + pair.shape)
    coefs = exchange(pair, "y")
    coefs = [coefs, swap(coefs, "c")]

    gamma = contract(own, cross, pieces)
    gamma = exchange(gamma.reshape(X * Y, ZL * ZH * PIECES, LANES), ("x", "y"))
    gamma = regroup(gamma.reshape(X * Y, ZL, ZH * PIECES, LANES))
    gamma = exchange(gamma.reshape(ZH * ZL, 2 * X, LANES), ("zh", "zl"))
    return transform(gamma, *coefs, nao)


def solution(mesh):
    split = Mesh(mesh.devices.reshape(X, ZL, C, Y, ZH), AXES)
    return jax.shard_map(
        on_device,
        mesh=split,
        in_specs=(P(("x", "zl", "c"), ("y", "zh")), P(("y", "zh"), ("x", "zl", "c")), P(("y", "zh"), None)),
        out_specs=P(None, AXES, None),
        check_vma=False,
    )
```
